32 devices in a mesh: owner: 4 (over y, x), batch: 8 (over z, core).
Axes of the slice: x: 2, y: 2, z: 4, core: 2. Of those that a mesh axis runs over, the one named last changes fastest.
Arguments:
- hidden: bfloat16 [512, 6144], P(('owner', 'batch')), may hold values from -6 to 6
- gains: float32 [2, 6144], replicated, may hold values from 0.25 to 1.75
- up_rows: bfloat16 [98304, 6144], P(('owner', 'batch')), may hold values from -0.078125 to 0.078125
- down_rows: bfloat16 [98304, 6144], P(('owner', 'batch')), may hold values from -0.1875 to 0.1875
- pick: int32 [4, 32], replicated, may hold values from 0 to 24, as said below
Outputs:
- final_rows: bfloat16 [512, 6144], P(('owner', 'batch'))
The draws below stay inside these ranges and needn't reach their ends.
Inputs may be any that keep to these rules, and one draw needn't show every extreme that they name: pick[g, u] names the one block among unit u's 24 blocks that row block g uses, or is 24 when it uses none of them. In every row block there is a lane of which every unit is used, and a unit that is not.
All inputs are finite; a program needn't handle non-finite values.
Results may differ from the reference program's by a relative error of at most 0.018.
Values may be sent and summed in bfloat16 or wider, within the bound.
A program may use at most 192 MiB of HBM per device.

```python
import jax
import jax.numpy as jnp
from jax import lax

D = 6144
FF = 49152
BLOCK = 128
LAYERS = 2
HELD = 24
GROUP_ROWS = 128
REQUESTS = 512
N_OWNER = 4
N_BATCH = 8
DEVICES = 32


def draw_pick(key, part):
    keys = jax.random.split(jax.random.fold_in(key, 17), 5)
    level = jax.random.randint(keys[0], (N_OWNER, 1), 1, 10)
    roll = jax.random.randint(keys[1], (N_OWNER, DEVICES), 0, 10)
    which = jax.random.randint(keys[2], (N_OWNER, DEVICES), 0, HELD)
    chosen = jnp.where(roll < level, which, HELD)
    unit_ids = jnp.arange(DEVICES)[None, :]
    full_lane = jax.random.randint(keys[3], (N_OWNER, 1), 0, N_BATCH)
    chosen = jnp.where(unit_ids % N_BATCH == full_lane, which, chosen)
    empty_lane = (full_lane + 1 + jax.random.randint(keys[4], (N_OWNER, 1), 0, N_BATCH - 1)) % N_BATCH
    chosen = jnp.where(unit_ids == empty_lane, HELD, chosen)
    return chosen.astype(jnp.int32)


def level_of(stream_key, shape, cuts, least, largest):
    gain, own = 1.0, jax.random.fold_in(stream_key, 6)
    for dim, parts in cuts:
        heights = jnp.exp(jax.random.uniform(jax.random.fold_in(own, dim), (parts,), jnp.float32, least / len(cuts), largest / len(cuts)))
        gain = gain * jnp.repeat(heights, shape[dim] // parts).reshape([-1 if axis == dim else 1 for axis in range(len(shape))])
    return gain


def bell_draw(own_key, dims, scale, most, cuts=(), dtype=jnp.bfloat16):
    level = level_of(own_key, dims, cuts, -0.22, 0.18) if cuts else 1.0
    entries = jax.random.normal(own_key, dims, jnp.float32) * scale * level
    return jnp.minimum(jnp.maximum(entries, -most), most).astype(dtype)


def setup_inputs(seed: int = 0) -> dict:
    key_list = jax.random.split(jax.random.key(seed), 6)
    hidden = bell_draw(key_list[0], (REQUESTS, D), 1.0, 6.0, ((0, 32),))
    gains = jnp.clip(1.0 + 0.15 * jax.random.normal(key_list[1], (LAYERS, D), jnp.float32), 0.25, 1.75)
    up_rows = bell_draw(key_list[2], (LAYERS * FF, D), D ** -0.5, 0.078125, ((0, 32),))
    down_rows = bell_draw(key_list[3], (LAYERS * FF, D), (DEVICES * BLOCK // 4) ** -0.5, 0.1875, ((0, 32),))
    pick = draw_pick(jax.random.fold_in(key_list[5], 71), 0)
    return {"hidden": hidden, "gains": gains, "up_rows": up_rows, "down_rows": down_rows, "pick": pick}


def normalize(rows_in, gain_row):
    values = rows_in.astype(jnp.float32)
    row_mean = lax.optimization_barrier(jnp.mean(values, axis=1, keepdims=True))
    centered = values - row_mean
    row_var = lax.optimization_barrier(jnp.mean(centered * centered, axis=1, keepdims=True))
    return (centered * lax.rsqrt(row_var + 1e-05) * gain_row[None, :]).astype(jnp.bfloat16)

def reference(hidden, gains, up_rows, down_rows, pick):
    dev_layer = DEVICES // LAYERS
    up_stack = up_rows.reshape(DEVICES * HELD, BLOCK, D)
    down_stack = down_rows.reshape(DEVICES * HELD, BLOCK, D)
    state = hidden
    for layer_at in range(LAYERS):
        normed = normalize(state, gains[layer_at])
        pieces = []
        for group_at in range(N_OWNER):
            units = (layer_at * dev_layer + jnp.arange(dev_layer)).astype(jnp.int32)
            chosen = pick[group_at, units]
            live_units = (chosen < HELD).astype(jnp.float32)
            selected = (units * HELD + jnp.minimum(chosen, HELD - 1)).astype(jnp.int32)
            up_sel = up_stack[selected].reshape(dev_layer * BLOCK, D)
            down_sel = down_stack[selected].astype(jnp.float32)
            group_rows = normed[group_at * GROUP_ROWS:(group_at + 1) * GROUP_ROWS]
            pre_act = jnp.dot(group_rows, up_sel.T, preferred_element_type=jnp.float32)
            neuron_mask = jnp.repeat(live_units, BLOCK)
            active = (jnp.maximum(pre_act, 0.0) * neuron_mask[None, :]).astype(jnp.bfloat16)
            active_four = active.astype(jnp.float32).reshape(GROUP_ROWS, dev_layer // N_BATCH, N_BATCH, BLOCK)
            down_four = down_sel.reshape(dev_layer // N_BATCH, N_BATCH, BLOCK, D)
            lane_terms = jnp.einsum('rjbk,jbkd->brd', active_four, down_four)
            lane_sum = lax.optimization_barrier(lane_terms.astype(jnp.bfloat16))
            pieces.append(lax.optimization_barrier(jnp.sum(lane_sum.astype(jnp.float32), axis=0)))
        update = jnp.concatenate(pieces, axis=0)
        state = (state.astype(jnp.float32) + update).astype(jnp.bfloat16)
    return state
```

```python
import functools

import jax
import jax.numpy as jnp
from jax import lax
from jax.experimental import pallas as pl
from jax.experimental.pallas import tpu as pltpu
from jax.sharding import PartitionSpec as P

BLOCK = 128
LAYERS = 2
CORES = 2
VMEM_BUDGET = 60 * 1024 * 1024
CHUNK = 1024


def layer_kernel(
    layer_at, owners, batches,
    state_ref, gains_ref, live_ref, up_hbm, down_hbm, out_ref,
    acts, up_v, down_v, part, core_in, x_in, x2_in, y_in, relay_in, z_in,
    wsem, zs, xs, ps, x2s, ys, yrs, ag_recv,
    cs, cr, rxs, rx2s, rys, ryrs, rzs, rxr, rx2r, ryr, ryrr, rzr,
):
    zn = batches // CORES
    per_layer = owners // LAYERS
    rows, width = state_ref.shape
    half = width // 2
    me_o = lax.axis_index("owner")
    me_b = lax.axis_index("batch")
    hi, lo = me_o // per_layer, me_o % per_layer
    zi, core = me_b // CORES, me_b % CORES
    peer_x = hi * per_layer + (1 - lo)
    peer_y = (1 - hi) * per_layer + lo
    diag = (1 - hi) * per_layer + (1 - lo)
    partner = zi * CORES + (1 - core)
    x_dev, y_dev, p_dev = (peer_x, me_b), (peer_y, me_b), (me_o, partner)
    in_layer = hi == layer_at

    def at_z(k):
        return (zi + k) % zn

    def z_dev(k):
        return (me_o, at_z(k) * CORES + core)

    def slot(z):
        return z * CORES + core

    def remote(src, dst, ssem, rsem, dev):
        return pltpu.make_async_remote_copy(
            src_ref=src, dst_ref=dst, send_sem=ssem, recv_sem=rsem,
            device_id=dev, device_id_type=pl.DeviceIdType.MESH)

    def piece(o, b, h):
        return acts.at[o, b, :, pl.ds(h * half, half)]

    def move(o, b, h, ssem, dev):
        return remote(piece(o, b, h), piece(o, b, h), ssem, ag_recv.at[o, b, h], dev)

    def arrive(o, b, h):
        move(o, b, h, zs.at[0, h], x_dev).wait_recv()

    @pl.when(in_layer)
    def _():
        pltpu.make_async_copy(up_hbm, up_v, wsem.at[0]).start()
        pltpu.make_async_copy(down_hbm, down_v, wsem.at[1]).start()

    values = state_ref[...].astype(jnp.float32)
    mean = jnp.mean(values, axis=1, keepdims=True)
    centered = values - mean
    var = jnp.mean(centered * centered, axis=1, keepdims=True)
    acts[me_o, me_b] = (
        centered * lax.rsqrt(var + 1e-05) * gains_ref[layer_at:layer_at + 1, :]
    ).astype(jnp.bfloat16)

    barrier = pltpu.get_barrier_semaphore()
    greeted = [x_dev, y_dev, p_dev] + [z_dev(k) for k in range(1, zn)]
    for dev in greeted:
        pl.semaphore_signal(barrier, inc=1, device_id=dev, device_id_type=pl.DeviceIdType.MESH)
    pl.semaphore_wait(barrier, len(greeted))

    for k in range(1, zn):
        for h in range(2):
            move(me_o, me_b, h, zs.at[k, h], z_dev(k)).start()

    @pl.when(in_layer)
    def _():
        def to_partner(o, k):
            for h in range(2):
                move(o, slot(at_z(k)), h, ps.at[o, k, h], p_dev).start()

        for t in range(zn + 2):
            if t < zn:
                b = slot(at_z(t))
                if t > 0:
                    for h in range(2):
                        arrive(me_o, b, h)
                for h in range(2):
                    move(me_o, b, h, xs.at[t, h], x_dev).start()
                to_partner(me_o, t)
            if 1 <= t <= zn:
                b = slot(at_z(t - 1))
                for h in range(2):
                    arrive(peer_y, b, h)
                move(peer_y, b, 1, x2s.at[t - 1], x_dev).start()
                to_partner(peer_y, t - 1)
            if t >= 2:
                b = slot(at_z(t - 2))
                for o in (peer_x, diag):
                    for h in range(2):
                        arrive(o, b, h)
                    to_partner(o, t - 2)

        for g in range(owners):
            for k in range(zn):
                for h in range(2):
                    arrive(g, at_z(k) * CORES + (1 - core), h)
        pltpu.make_async_copy(up_hbm, up_v, wsem.at[0]).wait()
        pltpu.make_async_copy(down_hbm, down_v, wsem.at[1]).wait()

        def give(g, k):
            z = at_z(k)
            return remote(part.at[g, z * CORES + (1 - core)], core_in.at[g, z], cs.at[g, k], cr.at[g, z], p_dev)

        def group(g, carry):
            flat = acts[g].reshape(batches * rows, width)
            pre = lax.dot_general(flat, up_v[g], (((1,), (1,)), ((), ())), preferred_element_type=jnp.float32)
            active = (jnp.maximum(pre, 0.0) * live_ref[pl.ds(g, 1), :]).astype(jnp.bfloat16)
            for at in range(0, width, CHUNK):
                cols = pl.ds(at, min(CHUNK, width - at))
                made = jnp.dot(active, down_v[g, :, cols], preferred_element_type=jnp.float32)
                part[g, :, :, cols] = made.astype(jnp.bfloat16).reshape(batches, rows, -1)
            for k in range(zn):
                give(g, k).start()
            return carry

        lax.fori_loop(0, owners, group, 0)

        def join(g, z, b):
            remote(part.at[g, b], core_in.at[g, z], cs.at[g, 0], cr.at[g, z], p_dev).wait_recv()
            core_in[g, z] = (core_in[g, z].astype(jnp.float32) + part[g, b].astype(jnp.float32)).astype(jnp.bfloat16)

        h2 = pl.ds(half, half)
        h1 = pl.ds(0, half)
        for k in range(zn):
            z = at_z(k)
            join(diag, z, slot(z))
            remote(core_in.at[diag, z, :, h2], x2_in.at[z], rx2s.at[k], rx2r.at[z], x_dev).start()
            remote(core_in.at[diag, z, :, h1], relay_in.at[z], ryrs.at[k], ryrr.at[z], y_dev).start()
        for k in range(zn):
            z = at_z(k)
            join(peer_y, z, slot(z))
            remote(core_in.at[peer_y, z, :, h1], y_in.at[z, :, h1], rys.at[k, 0], ryr.at[z, 0], y_dev).start()
            join(peer_x, z, slot(z))
            remote(core_in.at[peer_x, z], x_in.at[z], rxs.at[k], rxr.at[z], x_dev).start()
        for k in range(zn):
            z = at_z(k)
            remote(core_in.at[diag, z, :, h2], x2_in.at[z], rx2s.at[k], rx2r.at[z], x_dev).wait_recv()
            core_in[peer_y, z, :, half:] = (
                core_in[peer_y, z, :, half:].astype(jnp.float32) + x2_in[z].astype(jnp.float32)
            ).astype(jnp.bfloat16)
            remote(core_in.at[peer_y, z, :, h2], y_in.at[z, :, h2], rys.at[k, 1], ryr.at[z, 1], y_dev).start()
        for k in list(range(1, zn)) + [0]:
            z = at_z(k)
            join(me_o, z, slot(z))
            remote(core_in.at[peer_x, z], x_in.at[z], rxs.at[k], rxr.at[z], x_dev).wait_recv()
            x_in[z] = (x_in[z].astype(jnp.float32) + core_in[me_o, z].astype(jnp.float32)).astype(jnp.bfloat16)
            if k:
                remote(x_in.at[z], z_in.at[zi], rzs.at[k], rzr.at[zi], z_dev(k)).start()
        out_ref[...] = x_in[zi]

        for k in range(zn):
            z = at_z(k)
            for h in range(2):
                move(me_o, slot(z), h, xs.at[k, h], x_dev).wait_send()
                for o in range(owners):
                    move(o, slot(z), h, ps.at[o, k, h], p_dev).wait_send()
            move(peer_y, slot(z), 1, x2s.at[k], x_dev).wait_send()
            for g in range(owners):
                give(g, k).wait_send()
            remote(core_in.at[diag, z, :, h2], x2_in.at[z], rx2s.at[k], rx2r.at[z], x_dev).wait_send()
            remote(core_in.at[diag, z, :, h1], relay_in.at[z], ryrs.at[k], ryrr.at[z], y_dev).wait_send()
            remote(core_in.at[peer_x, z], x_in.at[z], rxs.at[k], rxr.at[z], x_dev).wait_send()
            remote(core_in.at[peer_y, z, :, h1], y_in.at[z, :, h1], rys.at[k, 0], ryr.at[z, 0], y_dev).wait_send()
            remote(core_in.at[peer_y, z, :, h2], y_in.at[z, :, h2], rys.at[k, 1], ryr.at[z, 1], y_dev).wait_send()

    @pl.when(jnp.logical_not(in_layer))
    def _():
        for t in range(zn + 1):
            if t < zn:
                b = slot(at_z(t))
                if t > 0:
                    for h in range(2):
                        arrive(me_o, b, h)
                move(me_o, b, 0, xs.at[t, 0], x_dev).start()
                for h in range(2):
                    move(me_o, b, h, ys.at[t, h], y_dev).start()
            if t >= 1:
                b = slot(at_z(t - 1))
                arrive(peer_x, b, 0)
                move(peer_x, b, 0, yrs.at[t - 1], y_dev).start()

        h2 = pl.ds(half, half)
        h1 = pl.ds(0, half)

        def pass_on(k, z):
            return remote(relay_in.at[z], x2_in.at[z], ryrs.at[k], rx2r.at[z], x_dev)

        order = list(range(1, zn)) + [0]
        for k in range(zn):
            z = at_z(k)
            remote(relay_in.at[z], relay_in.at[z], ryrs.at[k], ryrr.at[z], y_dev).wait_recv()
            pass_on(k, z).start()
        for k in order:
            z = at_z(k)
            remote(y_in.at[z, :, h1], y_in.at[z, :, h1], rys.at[k, 0], ryr.at[z, 0], y_dev).wait_recv()
            pass_on(k, z).wait_recv()
            y_in[z, :, :half] = (y_in[z, :, :half].astype(jnp.float32) + x2_in[z].astype(jnp.float32)).astype(jnp.bfloat16)
            remote(y_in.at[z, :, h2], y_in.at[z, :, h2], rys.at[k, 1], ryr.at[z, 1], y_dev).wait_recv()
            if k:
                remote(y_in.at[z], z_in.at[zi], rzs.at[k], rzr.at[zi], z_dev(k)).start()
        out_ref[...] = y_in[zi]

        for k in range(zn):
            z = at_z(k)
            b = slot(z)
            move(me_o, b, 0, xs.at[k, 0], x_dev).wait_send()
            for h in range(2):
                move(me_o, b, h, ys.at[k, h], y_dev).wait_send()
            move(peer_x, b, 0, yrs.at[k], y_dev).wait_send()
            pass_on(k, z).wait_send()

    total = values + out_ref[...].astype(jnp.float32)
    for k in range(1, zn):
        z = at_z(k)
        remote(x_in.at[z], z_in.at[z], rzs.at[k], rzr.at[z], z_dev(k)).wait_recv()
        total = total + z_in[z].astype(jnp.float32)
    out_ref[...] = total.astype(jnp.bfloat16)
    for k in range(1, zn):
        for h in range(2):
            move(me_o, me_b, h, zs.at[k, h], z_dev(k)).wait_send()
        remote(x_in.at[at_z(k)], z_in.at[zi], rzs.at[k], rzr.at[zi], z_dev(k)).wait_send()


def scratch_plan(owners, batches, rows, width):
    zn = batches // CORES
    half = width // 2
    bf = jnp.bfloat16
    return [
        ((owners, batches, rows, width), bf),
        ((owners, BLOCK, width), bf),
        ((owners, BLOCK, width), bf),
        ((owners, batches, rows, width), bf),
        ((owners, zn, rows, width), bf),
        ((zn, rows, width), bf),
        ((zn, rows, half), bf),
        ((zn, rows, width), bf),
        ((zn, rows, half), bf),
        ((zn, rows, width), bf),
    ]


def scratch_bytes(plan):
    total = 0
    for shape, kind in plan:
        size = jnp.dtype(kind).itemsize
        for extent in shape:
            size *= extent
        total += size
    return total


def run_layer(layer_at, owners, batches, state, gains, live, up_send, down_send):
    rows, width = state.shape
    zn = batches // CORES
    plan = scratch_plan(owners, batches, rows, width)
    dma = pltpu.SemaphoreType.DMA
    sems = [(2,), (zn, 2), (zn, 2), (owners, zn, 2), (zn,), (zn, 2), (zn,), (owners, batches, 2),
            (owners, zn), (owners, zn), (zn,), (zn,), (zn, 2), (zn,), (zn,),
            (zn,), (zn,), (zn, 2), (zn,), (zn,)]
    vmem = pl.BlockSpec(memory_space=pltpu.VMEM)
    hbm = pl.BlockSpec(memory_space=pl.ANY)
    return pl.pallas_call(
        functools.partial(layer_kernel, layer_at, owners, batches),
        out_shape=jax.ShapeDtypeStruct((rows, width), jnp.bfloat16),
        in_specs=[vmem, vmem, vmem, hbm, hbm],
        out_specs=vmem,
        scratch_shapes=[pltpu.VMEM(s, d) for s, d in plan] + [dma(s) for s in sems],
        compiler_params=pltpu.CompilerParams(
            collective_id=layer_at, has_side_effects=True, vmem_limit_bytes=VMEM_BUDGET),
        name=f"sublayer_{layer_at}",
    )(state, gains, live, up_send, down_send)


def stay_body(hidden, gains, up_rows, down_rows, pick):
    owners = lax.axis_size("owner")
    batches = lax.axis_size("batch")
    held_blocks = up_rows.shape[0] // BLOCK
    model_width = up_rows.shape[1]
    sender = lax.axis_index("owner") * batches + lax.axis_index("batch")
    my_picks = lax.dynamic_slice_in_dim(pick, sender, 1, 1)[:, 0]
    chosen = jnp.minimum(my_picks, held_blocks - 1)
    up_send = up_rows.reshape(held_blocks, BLOCK, model_width)[chosen]
    down_send = down_rows.reshape(held_blocks, BLOCK, model_width)[chosen]
    live = jnp.broadcast_to((my_picks < held_blocks).astype(jnp.float32)[:, None], (owners, BLOCK))
    state = hidden
    for layer_at in range(LAYERS):
        state = run_layer(layer_at, owners, batches, state, gains, live, up_send, down_send)
    return state


def normalize(rows_in, gain_row):
    values = rows_in.astype(jnp.float32)
    row_mean = jnp.mean(values, axis=1, keepdims=True)
    centered = values - row_mean
    row_var = jnp.mean(centered * centered, axis=1, keepdims=True)
    return (centered * lax.rsqrt(row_var + 1e-05) * gain_row[None, :]).astype(jnp.bfloat16)


def body(hidden, gains, up_rows, down_rows, pick):
    owners = lax.axis_size("owner")
    batches = lax.axis_size("batch")
    group_at = lax.axis_index("owner")
    lane_at = lax.axis_index("batch")
    held_blocks = up_rows.shape[0] // BLOCK
    model_width = up_rows.shape[1]
    local_rows = hidden.shape[0]
    sender = group_at * batches + lane_at
    my_picks = lax.dynamic_slice_in_dim(pick, sender, 1, 1)[:, 0]
    chosen = jnp.minimum(my_picks, held_blocks - 1)
    up_send = up_rows.reshape(held_blocks, BLOCK, model_width)[chosen]
    down_send = down_rows.reshape(held_blocks, BLOCK, model_width)[chosen]
    group_picks = lax.dynamic_slice_in_dim(pick, group_at, 1, 0)[0]
    live_slots = (group_picks[jnp.arange(owners) * batches + lane_at] < held_blocks).astype(
        jnp.float32
    )
    up_recv, down_recv = (
        lax.all_to_all(up_send, "owner", split_axis=0, concat_axis=0, tiled=True),
        lax.all_to_all(down_send, "owner", split_axis=0, concat_axis=0, tiled=True),
    )
    per_layer = owners // LAYERS
    residual = hidden
    for layer_at in range(LAYERS):
        first_slot = layer_at * per_layer
        up_part = up_recv[first_slot : first_slot + per_layer]
        down_part = down_recv[first_slot : first_slot + per_layer]
        keep_slots = live_slots[first_slot : first_slot + per_layer]
        up_flat = up_part.reshape(per_layer * BLOCK, model_width)
        down_flat = down_part.reshape(per_layer * BLOCK, model_width)
        neuron_mask = jnp.repeat(keep_slots, BLOCK)
        normed = normalize(residual, gains[layer_at])

        def expand(
            rows_piece,
            row_start,
            up_part=up_part,
            up_flat=up_flat,
            keep_slots=keep_slots,
            neuron_mask=neuron_mask,
        ):
            pre_act = lax.dot_general(
                rows_piece, up_flat, (((1,), (1,)), ((), ())), preferred_element_type=jnp.float32
            )
            return (jnp.maximum(pre_act, 0.0) * neuron_mask[None, :]).astype(jnp.bfloat16)

        active = expand(lax.all_gather(normed, "batch", axis=0, tiled=True), jnp.int32(0))

        def contract(
            row_start,
            row_count,
            active=active,
            down_part=down_part,
            down_flat=down_flat,
            keep_slots=keep_slots,
        ):
            return jnp.dot(active, down_flat, preferred_element_type=jnp.float32)

        summed = lax.psum_scatter(
            contract(jnp.int32(0), lax.axis_size("batch") * local_rows).astype(jnp.bfloat16),
            "batch",
            scatter_dimension=0,
            tiled=True,
        ).astype(jnp.float32)
        residual = (residual.astype(jnp.float32) + summed).astype(jnp.bfloat16)
    return residual


def solution(mesh):
    in_specs = (
        P(("owner", "batch"), None),
        P(),
        P(("owner", "batch"), None),
        P(("owner", "batch"), None),
        P(),
    )
    out_specs = P(("owner", "batch"), None)
    owners, batches = mesh.shape["owner"], mesh.shape["batch"]

    def whole(hidden, gains, up_rows, down_rows, pick):
        rows = hidden.shape[0] // (owners * batches)
        plan = scratch_plan(owners, batches, rows, hidden.shape[1])
        fits = owners == 2 * LAYERS and scratch_bytes(plan) * 5 < VMEM_BUDGET * 4
        chosen = stay_body if fits else body
        return jax.shard_map(chosen, mesh=mesh, in_specs=in_specs, out_specs=out_specs, check_vma=False)(
            hidden, gains, up_rows, down_rows, pick)

    return whole
```

```python
import functools

import jax
import jax.numpy as jnp
from jax import lax
from jax.experimental import pallas as pl
from jax.experimental.pallas import tpu as pltpu
from jax.sharding import PartitionSpec as P

BLOCK = 128
LAYERS = 2
CORES = 2
VMEM_BUDGET = 60 * 1024 * 1024
CHUNK = 1024


def layer_kernel(
    layer_at, owners, batches,
    state_ref, gains_ref, live_ref, up_hbm, down_hbm, out_ref,
    acts, up_v, down_v, part, core_in, x_in, x2_in, y_in, relay_in, z_in,
    wsem, zs, xs, ps, x2s, ys, yrs, ag_recv,
    cs, cr, rxs, rx2s, rys, ryrs, rzs, rxr, rx2r, ryr, ryrr, rzr,
):
    zn = batches // CORES
    per_layer = owners // LAYERS
    rows, width = state_ref.shape
    half = width // 2
    me_o = lax.axis_index("owner")
    me_b = lax.axis_index("batch")
    hi, lo = me_o // per_layer, me_o % per_layer
    zi, core = me_b // CORES, me_b % CORES
    peer_x = hi * per_layer + (1 - lo)
    peer_y = (1 - hi) * per_layer + lo
    diag = (1 - hi) * per_layer + (1 - lo)
    partner = zi * CORES + (1 - core)
    x_dev, y_dev, p_dev = (peer_x, me_b), (peer_y, me_b), (me_o, partner)
    in_layer = hi == layer_at

    def at_z(k):
        return (zi + k) % zn

    def z_dev(k):
        return (me_o, at_z(k) * CORES + core)

    def slot(z):
        return z * CORES + core

    def remote(src, dst, ssem, rsem, dev):
        return pltpu.make_async_remote_copy(
            src_ref=src, dst_ref=dst, send_sem=ssem, recv_sem=rsem,
            device_id=dev, device_id_type=pl.DeviceIdType.MESH)

    def piece(o, b, h):
        return acts.at[o, b, :, pl.ds(h * half, half)]

    def move(o, b, h, ssem, dev):
        return remote(piece(o, b, h), piece(o, b, h), ssem, ag_recv.at[o, b, h], dev)

    def arrive(o, b, h):
        move(o, b, h, zs.at[0, h], x_dev).wait_recv()

    @pl.when(in_layer)
    def _():
        pltpu.make_async_copy(up_hbm, up_v, wsem.at[0]).start()
        pltpu.make_async_copy(down_hbm, down_v, wsem.at[1]).start()

    values = state_ref[...].astype(jnp.float32)
    mean = jnp.mean(values, axis=1, keepdims=True)
    centered = values - mean
    var = jnp.mean(centered * centered, axis=1, keepdims=True)
    acts[me_o, me_b] = (
        centered * lax.rsqrt(var + 1e-05) * gains_ref[layer_at:layer_at + 1, :]
    ).astype(jnp.bfloat16)

    barrier = pltpu.get_barrier_semaphore()
    greeted = [x_dev, y_dev, p_dev] + [z_dev(k) for k in range(1, zn)]
    for dev in greeted:
        pl.semaphore_signal(barrier, inc=1, device_id=dev, device_id_type=pl.DeviceIdType.MESH)
    pl.semaphore_wait(barrier, len(greeted))

    for k in range(1, zn):
        for h in range(2):
            move(me_o, me_b, h, zs.at[k, h], z_dev(k)).start()

    @pl.when(in_layer)
    def _():
        def to_partner(o, k):
            for h in range(2):
                move(o, slot(at_z(k)), h, ps.at[o, k, h], p_dev).start()

        for t in range(zn + 1):
            if t < zn:
                b = slot(at_z(t))
                if t > 0:
                    for h in range(2):
                        arrive(me_o, b, h)
                for h in range(2):
                    move(me_o, b, h, xs.at[t, h], x_dev).start()
                to_partner(me_o, t)
            if t >= 1:
                b = slot(at_z(t - 1))
                for h in (1, 0):
                    arrive(peer_y, b, h)
                    if h == 1:
                        move(peer_y, b, 1, x2s.at[t - 1], x_dev).start()
                to_partner(peer_y, t - 1)

        def give(g, k):
            z = at_z(k)
            return remote(part.at[g, z * CORES + (1 - core)], core_in.at[g, z], cs.at[g, k], cr.at[g, z], p_dev)

        def group(g):
            for k in range(zn):
                for h in range(2):
                    arrive(g, at_z(k) * CORES + (1 - core), h)
            flat = acts[g].reshape(batches * rows, width)
            pre = lax.dot_general(flat, up_v[g], (((1,), (1,)), ((), ())), preferred_element_type=jnp.float32)
            active = (jnp.maximum(pre, 0.0) * live_ref[pl.ds(g, 1), :]).astype(jnp.bfloat16)
            for at in range(0, width, CHUNK):
                cols = pl.ds(at, min(CHUNK, width - at))
                made = jnp.dot(active, down_v[g, :, cols], preferred_element_type=jnp.float32)
                part[g, :, :, cols] = made.astype(jnp.bfloat16).reshape(batches, rows, -1)
            for k in range(zn):
                give(g, k).start()

        def join(g, z, b):
            remote(part.at[g, b], core_in.at[g, z], cs.at[g, 0], cr.at[g, z], p_dev).wait_recv()
            core_in[g, z] = (core_in[g, z].astype(jnp.float32) + part[g, b].astype(jnp.float32)).astype(jnp.bfloat16)

        pltpu.make_async_copy(up_hbm, up_v, wsem.at[0]).wait()
        pltpu.make_async_copy(down_hbm, down_v, wsem.at[1]).wait()
        group(me_o)
        for k in range(zn):
            for o in (diag, peer_x):
                for h in range(2):
                    arrive(o, slot(at_z(k)), h)
                to_partner(o, k)
        group(peer_y)
        group(diag)
        h2 = pl.ds(half, half)
        h1 = pl.ds(0, half)
        for k in range(zn):
            z = at_z(k)
            join(diag, z, slot(z))
            remote(core_in.at[diag, z, :, h2], x2_in.at[z], rx2s.at[k], rx2r.at[z], x_dev).start()
            remote(core_in.at[diag, z, :, h1], relay_in.at[z], ryrs.at[k], ryrr.at[z], y_dev).start()
            join(peer_y, z, slot(z))
            remote(core_in.at[peer_y, z, :, h1], y_in.at[z, :, h1], rys.at[k, 0], ryr.at[z, 0], y_dev).start()
        group(peer_x)
        for k in range(zn):
            z = at_z(k)
            remote(core_in.at[diag, z, :, h2], x2_in.at[z], rx2s.at[k], rx2r.at[z], x_dev).wait_recv()
            core_in[peer_y, z, :, half:] = (
                core_in[peer_y, z, :, half:].astype(jnp.float32) + x2_in[z].astype(jnp.float32)
            ).astype(jnp.bfloat16)
            remote(core_in.at[peer_y, z, :, h2], y_in.at[z, :, h2], rys.at[k, 1], ryr.at[z, 1], y_dev).start()
        for k in list(range(1, zn)) + [0]:
            z = at_z(k)
            join(peer_x, z, slot(z))
            remote(core_in.at[peer_x, z], x_in.at[z], rxs.at[k], rxr.at[z], x_dev).start()
        for k in list(range(1, zn)) + [0]:
            z = at_z(k)
            join(me_o, z, slot(z))
            remote(core_in.at[peer_x, z], x_in.at[z], rxs.at[k], rxr.at[z], x_dev).wait_recv()
            x_in[z] = (x_in[z].astype(jnp.float32) + core_in[me_o, z].astype(jnp.float32)).astype(jnp.bfloat16)
            if k:
                remote(x_in.at[z], z_in.at[zi], rzs.at[k], rzr.at[zi], z_dev(k)).start()
        out_ref[...] = x_in[zi]

        for k in range(zn):
            z = at_z(k)
            for h in range(2):
                move(me_o, slot(z), h, xs.at[k, h], x_dev).wait_send()
                for o in range(owners):
                    move(o, slot(z), h, ps.at[o, k, h], p_dev).wait_send()
            move(peer_y, slot(z), 1, x2s.at[k], x_dev).wait_send()
            for g in range(owners):
                give(g, k).wait_send()
            remote(core_in.at[diag, z, :, h2], x2_in.at[z], rx2s.at[k], rx2r.at[z], x_dev).wait_send()
            remote(core_in.at[diag, z, :, h1], relay_in.at[z], ryrs.at[k], ryrr.at[z], y_dev).wait_send()
            remote(core_in.at[peer_x, z], x_in.at[z], rxs.at[k], rxr.at[z], x_dev).wait_send()
            remote(core_in.at[peer_y, z, :, h1], y_in.at[z, :, h1], rys.at[k, 0], ryr.at[z, 0], y_dev).wait_send()
            remote(core_in.at[peer_y, z, :, h2], y_in.at[z, :, h2], rys.at[k, 1], ryr.at[z, 1], y_dev).wait_send()

    @pl.when(jnp.logical_not(in_layer))
    def _():
        for t in range(zn + 1):
            if t < zn:
                b = slot(at_z(t))
                if t > 0:
                    for h in range(2):
                        arrive(me_o, b, h)
                move(me_o, b, 0, xs.at[t, 0], x_dev).start()
                for h in range(2):
                    move(me_o, b, h, ys.at[t, h], y_dev).start()
            if t >= 1:
                b = slot(at_z(t - 1))
                arrive(peer_x, b, 0)
                move(peer_x, b, 0, yrs.at[t - 1], y_dev).start()

        h2 = pl.ds(half, half)
        h1 = pl.ds(0, half)

        def pass_on(k, z):
            return remote(relay_in.at[z], x2_in.at[z], ryrs.at[k], rx2r.at[z], x_dev)

        order = list(range(1, zn)) + [0]
        for k in range(zn):
            z = at_z(k)
            remote(relay_in.at[z], relay_in.at[z], ryrs.at[k], ryrr.at[z], y_dev).wait_recv()
            pass_on(k, z).start()
        for k in order:
            z = at_z(k)
            remote(y_in.at[z, :, h1], y_in.at[z, :, h1], rys.at[k, 0], ryr.at[z, 0], y_dev).wait_recv()
            pass_on(k, z).wait_recv()
            y_in[z, :, :half] = (y_in[z, :, :half].astype(jnp.float32) + x2_in[z].astype(jnp.float32)).astype(jnp.bfloat16)
            remote(y_in.at[z, :, h2], y_in.at[z, :, h2], rys.at[k, 1], ryr.at[z, 1], y_dev).wait_recv()
            if k:
                remote(y_in.at[z], z_in.at[zi], rzs.at[k], rzr.at[zi], z_dev(k)).start()
        out_ref[...] = y_in[zi]

        for k in range(zn):
            z = at_z(k)
            b = slot(z)
            move(me_o, b, 0, xs.at[k, 0], x_dev).wait_send()
            for h in range(2):
                move(me_o, b, h, ys.at[k, h], y_dev).wait_send()
            move(peer_x, b, 0, yrs.at[k], y_dev).wait_send()
            pass_on(k, z).wait_send()

    total = values + out_ref[...].astype(jnp.float32)
    for k in range(1, zn):
        z = at_z(k)
        remote(x_in.at[z], z_in.at[z], rzs.at[k], rzr.at[z], z_dev(k)).wait_recv()
        total = total + z_in[z].astype(jnp.float32)
    out_ref[...] = total.astype(jnp.bfloat16)
    for k in range(1, zn):
        for h in range(2):
            move(me_o, me_b, h, zs.at[k, h], z_dev(k)).wait_send()
        remote(x_in.at[at_z(k)], z_in.at[zi], rzs.at[k], rzr.at[zi], z_dev(k)).wait_send()


def scratch_plan(owners, batches, rows, width):
    zn = batches // CORES
    half = width // 2
    bf = jnp.bfloat16
    return [
        ((owners, batches, rows, width), bf),
        ((owners, BLOCK, width), bf),
        ((owners, BLOCK, width), bf),
        ((owners, batches, rows, width), bf),
        ((owners, zn, rows, width), bf),
        ((zn, rows, width), bf),
        ((zn, rows, half), bf),
        ((zn, rows, width), bf),
        ((zn, rows, half), bf),
        ((zn, rows, width), bf),
    ]


def scratch_bytes(plan):
    total = 0
    for shape, kind in plan:
        size = jnp.dtype(kind).itemsize
        for extent in shape:
            size *= extent
        total += size
    return total


def run_layer(layer_at, owners, batches, state, gains, live, up_send, down_send):
    rows, width = state.shape
    zn = batches // CORES
    plan = scratch_plan(owners, batches, rows, width)
    dma = pltpu.SemaphoreType.DMA
    sems = [(2,), (zn, 2), (zn, 2), (owners, zn, 2), (zn,), (zn, 2), (zn,), (owners, batches, 2),
            (owners, zn), (owners, zn), (zn,), (zn,), (zn, 2), (zn,), (zn,),
            (zn,), (zn,), (zn, 2), (zn,), (zn,)]
    vmem = pl.BlockSpec(memory_space=pltpu.VMEM)
    hbm = pl.BlockSpec(memory_space=pl.ANY)
    return pl.pallas_call(
        functools.partial(layer_kernel, layer_at, owners, batches),
        out_shape=jax.ShapeDtypeStruct((rows, width), jnp.bfloat16),
        in_specs=[vmem, vmem, vmem, hbm, hbm],
        out_specs=vmem,
        scratch_shapes=[pltpu.VMEM(s, d) for s, d in plan] + [dma(s) for s in sems],
        compiler_params=pltpu.CompilerParams(
            collective_id=layer_at, has_side_effects=True, vmem_limit_bytes=VMEM_BUDGET),
        name=f"sublayer_{layer_at}",
    )(state, gains, live, up_send, down_send)


def fetch_kernel(owners, batches, held, pick_ref, up_ref, down_ref, live_ref, up_out, down_out, buf, isem, osem):
    sender = lax.axis_index("owner") * batches + lax.axis_index("batch")

    def read(i):
        g = i % owners
        at = jnp.minimum(pick_ref[g, sender], held - 1)
        src = up_ref if i < owners else down_ref
        return pltpu.make_async_copy(src.at[at], buf.at[i], isem.at[i])

    def write(i):
        dst = up_out if i < owners else down_out
        return pltpu.make_async_copy(buf.at[i], dst.at[i % owners], osem.at[i])

    for i in range(2 * owners):
        read(i).start()
    for g in range(owners):
        live = (pick_ref[g, sender] < held).astype(jnp.float32)
        live_ref[g:g + 1, :] = jnp.full((1, BLOCK), live, jnp.float32)
    for i in range(2 * owners):
        read(i).wait()
        write(i).start()
    for i in range(2 * owners):
        write(i).wait()


def fetch(owners, batches, up_rows, down_rows, pick):
    width = up_rows.shape[1]
    held = up_rows.shape[0] // BLOCK
    hbm = pl.BlockSpec(memory_space=pl.ANY)
    sent = jax.ShapeDtypeStruct((owners, BLOCK, width), up_rows.dtype)
    return pl.pallas_call(
        functools.partial(fetch_kernel, owners, batches, held),
        out_shape=(jax.ShapeDtypeStruct((owners, BLOCK), jnp.float32), sent, sent),
        in_specs=[pl.BlockSpec(memory_space=pltpu.SMEM), hbm, hbm],
        out_specs=(pl.BlockSpec(memory_space=pltpu.VMEM), hbm, hbm),
        scratch_shapes=[
            pltpu.VMEM((2 * owners, BLOCK, width), up_rows.dtype),
            pltpu.SemaphoreType.DMA((2 * owners,)),
            pltpu.SemaphoreType.DMA((2 * owners,)),
        ],
        compiler_params=pltpu.CompilerParams(vmem_limit_bytes=VMEM_BUDGET),
        name="fetch",
    )(pick, up_rows.reshape(held, BLOCK, width), down_rows.reshape(held, BLOCK, width))


def stay_body(hidden, gains, up_rows, down_rows, pick):
    owners = lax.axis_size("owner")
    batches = lax.axis_size("batch")
    live, up_send, down_send = fetch(owners, batches, up_rows, down_rows, pick)
    state = hidden
    for layer_at in range(LAYERS):
        state = run_layer(layer_at, owners, batches, state, gains, live, up_send, down_send)
    return state


def normalize(rows_in, gain_row):
    values = rows_in.astype(jnp.float32)
    row_mean = jnp.mean(values, axis=1, keepdims=True)
    centered = values - row_mean
    row_var = jnp.mean(centered * centered, axis=1, keepdims=True)
    return (centered * lax.rsqrt(row_var + 1e-05) * gain_row[None, :]).astype(jnp.bfloat16)


def body(hidden, gains, up_rows, down_rows, pick):
    owners = lax.axis_size("owner")
    batches = lax.axis_size("batch")
    group_at = lax.axis_index("owner")
    lane_at = lax.axis_index("batch")
    held_blocks = up_rows.shape[0] // BLOCK
    model_width = up_rows.shape[1]
    local_rows = hidden.shape[0]
    sender = group_at * batches + lane_at
    my_picks = lax.dynamic_slice_in_dim(pick, sender, 1, 1)[:, 0]
    chosen = jnp.minimum(my_picks, held_blocks - 1)
    up_send = up_rows.reshape(held_blocks, BLOCK, model_width)[chosen]
    down_send = down_rows.reshape(held_blocks, BLOCK, model_width)[chosen]
    group_picks = lax.dynamic_slice_in_dim(pick, group_at, 1, 0)[0]
    live_slots = (group_picks[jnp.arange(owners) * batches + lane_at] < held_blocks).astype(
        jnp.float32
    )
    up_recv, down_recv = (
        lax.all_to_all(up_send, "owner", split_axis=0, concat_axis=0, tiled=True),
        lax.all_to_all(down_send, "owner", split_axis=0, concat_axis=0, tiled=True),
    )
    per_layer = owners // LAYERS
    residual = hidden
    for layer_at in range(LAYERS):
        first_slot = layer_at * per_layer
        up_part = up_recv[first_slot : first_slot + per_layer]
        down_part = down_recv[first_slot : first_slot + per_layer]
        keep_slots = live_slots[first_slot : first_slot + per_layer]
        up_flat = up_part.reshape(per_layer * BLOCK, model_width)
        down_flat = down_part.reshape(per_layer * BLOCK, model_width)
        neuron_mask = jnp.repeat(keep_slots, BLOCK)
        normed = normalize(residual, gains[layer_at])

        def expand(
            rows_piece,
            row_start,
            up_part=up_part,
            up_flat=up_flat,
            keep_slots=keep_slots,
            neuron_mask=neuron_mask,
        ):
            pre_act = lax.dot_general(
                rows_piece, up_flat, (((1,), (1,)), ((), ())), preferred_element_type=jnp.float32
            )
            return (jnp.maximum(pre_act, 0.0) * neuron_mask[None, :]).astype(jnp.bfloat16)

        active = expand(lax.all_gather(normed, "batch", axis=0, tiled=True), jnp.int32(0))

        def contract(
            row_start,
            row_count,
            active=active,
            down_part=down_part,
            down_flat=down_flat,
            keep_slots=keep_slots,
        ):
            return jnp.dot(active, down_flat, preferred_element_type=jnp.float32)

        summed = lax.psum_scatter(
            contract(jnp.int32(0), lax.axis_size("batch") * local_rows).astype(jnp.bfloat16),
            "batch",
            scatter_dimension=0,
            tiled=True,
        ).astype(jnp.float32)
        residual = (residual.astype(jnp.float32) + summed).astype(jnp.bfloat16)
    return residual


def solution(mesh):
    in_specs = (
        P(("owner", "batch"), None),
        P(),
        P(("owner", "batch"), None),
        P(("owner", "batch"), None),
        P(),
    )
    out_specs = P(("owner", "batch"), None)
    owners, batches = mesh.shape["owner"], mesh.shape["batch"]

    def whole(hidden, gains, up_rows, down_rows, pick):
        rows = hidden.shape[0] // (owners * batches)
        plan = scratch_plan(owners, batches, rows, hidden.shape[1])
        fits = owners == 2 * LAYERS and scratch_bytes(plan) * 5 < VMEM_BUDGET * 4
        chosen = stay_body if fits else body
        return jax.shard_map(chosen, mesh=mesh, in_specs=in_specs, out_specs=out_specs, check_vma=False)(
            hidden, gains, up_rows, down_rows, pick)

    return whole
```

```python
import functools

import jax
import jax.numpy as jnp
from jax import lax
from jax.experimental import pallas as pl
from jax.experimental.pallas import tpu as pltpu
from jax.sharding import PartitionSpec as P

BLOCK = 128
LAYERS = 2
CORES = 2
VMEM_BUDGET = 60 * 1024 * 1024
CHUNK = 1024


def layer_kernel(
    layer_at, owners, batches,
    state_ref, gains_ref, live_ref, up_hbm, down_hbm, out_ref,
    acts, up_v, down_v, part, core_in, x_in, x2_in, y_in, relay_in, z_in,
    wsem, zs, xs, ps, x2s, ys, yrs, ag_recv,
    cs, cr, rxs, rx2s, rys, ryrs, rzs, rxr, rx2r, ryr, ryrr, rzr,
):
    zn = batches // CORES
    per_layer = owners // LAYERS
    rows, width = state_ref.shape
    half = width // 2
    me_o = lax.axis_index("owner")
    me_b = lax.axis_index("batch")
    hi, lo = me_o // per_layer, me_o % per_layer
    zi, core = me_b // CORES, me_b % CORES
    peer_x = hi * per_layer + (1 - lo)
    peer_y = (1 - hi) * per_layer + lo
    diag = (1 - hi) * per_layer + (1 - lo)
    partner = zi * CORES + (1 - core)
    x_dev, y_dev, p_dev = (peer_x, me_b), (peer_y, me_b), (me_o, partner)
    in_layer = hi == layer_at

    def at_z(k):
        if zn & (zn - 1):
            return (zi + k) % zn
        found, bit = 0, 1
        while bit < zn:
            found = found + ((zi // bit + k // bit) % 2) * bit
            bit *= 2
        return found

    back = list(range(zn - 1, -1, -1))

    def z_dev(k):
        return (me_o, at_z(k) * CORES + core)

    def slot(z):
        return z * CORES + core

    def remote(src, dst, ssem, rsem, dev):
        return pltpu.make_async_remote_copy(
            src_ref=src, dst_ref=dst, send_sem=ssem, recv_sem=rsem,
            device_id=dev, device_id_type=pl.DeviceIdType.MESH)

    def piece(o, b, h):
        return acts.at[o, b, :, pl.ds(h * half, half)]

    def move(o, b, h, ssem, dev):
        return remote(piece(o, b, h), piece(o, b, h), ssem, ag_recv.at[o, b, h], dev)

    def arrive(o, b, h):
        move(o, b, h, zs.at[0, h], x_dev).wait_recv()

    @pl.when(in_layer)
    def _():
        pltpu.make_async_copy(up_hbm, up_v, wsem.at[0]).start()
        pltpu.make_async_copy(down_hbm, down_v, wsem.at[1]).start()

    values = state_ref[...].astype(jnp.float32)
    mean = jnp.mean(values, axis=1, keepdims=True)
    centered = values - mean
    var = jnp.mean(centered * centered, axis=1, keepdims=True)
    acts[me_o, me_b] = (
        centered * lax.rsqrt(var + 1e-05) * gains_ref[layer_at:layer_at + 1, :]
    ).astype(jnp.bfloat16)

    barrier = pltpu.get_barrier_semaphore()
    greeted = [x_dev, y_dev, p_dev] + [z_dev(k) for k in range(1, zn)]
    for dev in greeted:
        pl.semaphore_signal(barrier, inc=1, device_id=dev, device_id_type=pl.DeviceIdType.MESH)
    pl.semaphore_wait(barrier, len(greeted))

    for k in range(1, zn):
        for h in range(2):
            move(me_o, me_b, h, zs.at[k, h], z_dev(k)).start()

    @pl.when(in_layer)
    def _():
        def to_partner(o, k):
            for h in range(2):
                move(o, slot(at_z(k)), h, ps.at[o, k, h], p_dev).start()

        for t in range(zn + 1):
            if t < zn:
                b = slot(at_z(t))
                if t > 0:
                    for h in range(2):
                        arrive(me_o, b, h)
                for h in range(2):
                    move(me_o, b, h, xs.at[t, h], x_dev).start()
                to_partner(me_o, t)
            if t >= 1:
                b = slot(at_z(t - 1))
                for h in (1, 0):
                    arrive(peer_y, b, h)
                    if h == 1:
                        move(peer_y, b, 1, x2s.at[t - 1], x_dev).start()
                to_partner(peer_y, t - 1)

        def give(g, k):
            z = at_z(k)
            return remote(part.at[g, z * CORES + (1 - core)], core_in.at[g, z], cs.at[g, k], cr.at[g, z], p_dev)

        def group(g):
            for k in range(zn):
                for h in range(2):
                    arrive(g, at_z(k) * CORES + (1 - core), h)
            flat = acts[g].reshape(batches * rows, width)
            pre = lax.dot_general(flat, up_v[g], (((1,), (1,)), ((), ())), preferred_element_type=jnp.float32)
            active = (jnp.maximum(pre, 0.0) * live_ref[pl.ds(g, 1), :]).astype(jnp.bfloat16)
            for at in range(0, width, CHUNK):
                cols = pl.ds(at, min(CHUNK, width - at))
                made = jnp.dot(active, down_v[g, :, cols], preferred_element_type=jnp.float32)
                part[g, :, :, cols] = made.astype(jnp.bfloat16).reshape(batches, rows, -1)
            for k in range(zn):
                give(g, k).start()

        def join(g, z, b):
            remote(part.at[g, b], core_in.at[g, z], cs.at[g, 0], cr.at[g, z], p_dev).wait_recv()
            core_in[g, z] = (core_in[g, z].astype(jnp.float32) + part[g, b].astype(jnp.float32)).astype(jnp.bfloat16)

        pltpu.make_async_copy(up_hbm, up_v, wsem.at[0]).wait()
        pltpu.make_async_copy(down_hbm, down_v, wsem.at[1]).wait()
        group(me_o)
        for k in range(zn):
            for o in (diag, peer_x):
                for h in range(2):
                    arrive(o, slot(at_z(k)), h)
                to_partner(o, k)
        group(peer_y)
        group(diag)
        h2 = pl.ds(half, half)
        h1 = pl.ds(0, half)
        for k in back:
            z = at_z(k)
            join(diag, z, slot(z))
            remote(core_in.at[diag, z, :, h2], x2_in.at[z], rx2s.at[k], rx2r.at[z], x_dev).start()
            remote(core_in.at[diag, z, :, h1], relay_in.at[z], ryrs.at[k], ryrr.at[z], y_dev).start()
            join(peer_y, z, slot(z))
            remote(core_in.at[peer_y, z, :, h1], y_in.at[z, :, h1], rys.at[k, 0], ryr.at[z, 0], y_dev).start()
        group(peer_x)
        for k in back:
            z = at_z(k)
            remote(core_in.at[diag, z, :, h2], x2_in.at[z], rx2s.at[k], rx2r.at[z], x_dev).wait_recv()
            core_in[peer_y, z, :, half:] = (
                core_in[peer_y, z, :, half:].astype(jnp.float32) + x2_in[z].astype(jnp.float32)
            ).astype(jnp.bfloat16)
            remote(core_in.at[peer_y, z, :, h2], y_in.at[z, :, h2], rys.at[k, 1], ryr.at[z, 1], y_dev).start()
        for k in back:
            z = at_z(k)
            join(peer_x, z, slot(z))
            remote(core_in.at[peer_x, z], x_in.at[z], rxs.at[k], rxr.at[z], x_dev).start()
        for k in back:
            z = at_z(k)
            join(me_o, z, slot(z))
            remote(core_in.at[peer_x, z], x_in.at[z], rxs.at[k], rxr.at[z], x_dev).wait_recv()
            x_in[z] = (x_in[z].astype(jnp.float32) + core_in[me_o, z].astype(jnp.float32)).astype(jnp.bfloat16)
            if k:
                remote(x_in.at[z], z_in.at[zi], rzs.at[k], rzr.at[zi], z_dev(k)).start()
        out_ref[...] = x_in[zi]

        for k in range(zn):
            z = at_z(k)
            for h in range(2):
                move(me_o, slot(z), h, xs.at[k, h], x_dev).wait_send()
                for o in range(owners):
                    move(o, slot(z), h, ps.at[o, k, h], p_dev).wait_send()
            move(peer_y, slot(z), 1, x2s.at[k], x_dev).wait_send()
            for g in range(owners):
                give(g, k).wait_send()
            remote(core_in.at[diag, z, :, h2], x2_in.at[z], rx2s.at[k], rx2r.at[z], x_dev).wait_send()
            remote(core_in.at[diag, z, :, h1], relay_in.at[z], ryrs.at[k], ryrr.at[z], y_dev).wait_send()
            remote(core_in.at[peer_x, z], x_in.at[z], rxs.at[k], rxr.at[z], x_dev).wait_send()
            remote(core_in.at[peer_y, z, :, h1], y_in.at[z, :, h1], rys.at[k, 0], ryr.at[z, 0], y_dev).wait_send()
            remote(core_in.at[peer_y, z, :, h2], y_in.at[z, :, h2], rys.at[k, 1], ryr.at[z, 1], y_dev).wait_send()

    @pl.when(jnp.logical_not(in_layer))
    def _():
        for t in range(zn + 1):
            if t < zn:
                b = slot(at_z(t))
                if t > 0:
                    for h in range(2):
                        arrive(me_o, b, h)
                move(me_o, b, 0, xs.at[t, 0], x_dev).start()
                for h in range(2):
                    move(me_o, b, h, ys.at[t, h], y_dev).start()
            if t >= 1:
                b = slot(at_z(t - 1))
                arrive(peer_x, b, 0)
                move(peer_x, b, 0, yrs.at[t - 1], y_dev).start()

        h2 = pl.ds(half, half)
        h1 = pl.ds(0, half)

        def pass_on(k, z):
            return remote(relay_in.at[z], x2_in.at[z], ryrs.at[k], rx2r.at[z], x_dev)

        for k in back:
            z = at_z(k)
            remote(relay_in.at[z], relay_in.at[z], ryrs.at[k], ryrr.at[z], y_dev).wait_recv()
            pass_on(k, z).start()
        for k in back:
            z = at_z(k)
            remote(y_in.at[z, :, h1], y_in.at[z, :, h1], rys.at[k, 0], ryr.at[z, 0], y_dev).wait_recv()
            pass_on(k, z).wait_recv()
            y_in[z, :, :half] = (y_in[z, :, :half].astype(jnp.float32) + x2_in[z].astype(jnp.float32)).astype(jnp.bfloat16)
            remote(y_in.at[z, :, h2], y_in.at[z, :, h2], rys.at[k, 1], ryr.at[z, 1], y_dev).wait_recv()
            if k:
                remote(y_in.at[z], z_in.at[zi], rzs.at[k], rzr.at[zi], z_dev(k)).start()
        out_ref[...] = y_in[zi]

        for k in range(zn):
            z = at_z(k)
            b = slot(z)
            move(me_o, b, 0, xs.at[k, 0], x_dev).wait_send()
            for h in range(2):
                move(me_o, b, h, ys.at[k, h], y_dev).wait_send()
            move(peer_x, b, 0, yrs.at[k], y_dev).wait_send()
            pass_on(k, z).wait_send()

    total = values + out_ref[...].astype(jnp.float32)
    for k in range(1, zn):
        z = at_z(k)
        remote(x_in.at[z], z_in.at[z], rzs.at[k], rzr.at[z], z_dev(k)).wait_recv()
        total = total + z_in[z].astype(jnp.float32)
    out_ref[...] = total.astype(jnp.bfloat16)
    for k in range(1, zn):
        for h in range(2):
            move(me_o, me_b, h, zs.at[k, h], z_dev(k)).wait_send()
        remote(x_in.at[at_z(k)], z_in.at[zi], rzs.at[k], rzr.at[zi], z_dev(k)).wait_send()


def scratch_plan(owners, batches, rows, width):
    zn = batches // CORES
    half = width // 2
    bf = jnp.bfloat16
    return [
        ((owners, batches, rows, width), bf),
        ((owners, BLOCK, width), bf),
        ((owners, BLOCK, width), bf),
        ((owners, batches, rows, width), bf),
        ((owners, zn, rows, width), bf),
        ((zn, rows, width), bf),
        ((zn, rows, half), bf),
        ((zn, rows, width), bf),
        ((zn, rows, half), bf),
        ((zn, rows, width), bf),
    ]


def scratch_bytes(plan):
    total = 0
    for shape, kind in plan:
        size = jnp.dtype(kind).itemsize
        for extent in shape:
            size *= extent
        total += size
    return total


def run_layer(layer_at, owners, batches, state, gains, live, up_send, down_send):
    rows, width = state.shape
    zn = batches // CORES
    plan = scratch_plan(owners, batches, rows, width)
    dma = pltpu.SemaphoreType.DMA
    sems = [(2,), (zn, 2), (zn, 2), (owners, zn, 2), (zn,), (zn, 2), (zn,), (owners, batches, 2),
            (owners, zn), (owners, zn), (zn,), (zn,), (zn, 2), (zn,), (zn,),
            (zn,), (zn,), (zn, 2), (zn,), (zn,)]
    vmem = pl.BlockSpec(memory_space=pltpu.VMEM)
    hbm = pl.BlockSpec(memory_space=pl.ANY)
    return pl.pallas_call(
        functools.partial(layer_kernel, layer_at, owners, batches),
        out_shape=jax.ShapeDtypeStruct((rows, width), jnp.bfloat16),
        in_specs=[vmem, vmem, vmem, hbm, hbm],
        out_specs=vmem,
        scratch_shapes=[pltpu.VMEM(s, d) for s, d in plan] + [dma(s) for s in sems],
        compiler_params=pltpu.CompilerParams(
            collective_id=layer_at, has_side_effects=True, vmem_limit_bytes=VMEM_BUDGET),
        name=f"sublayer_{layer_at}",
    )(state, gains, live, up_send, down_send)


def fetch_kernel(owners, batches, held, pick_ref, up_ref, down_ref, live_ref, up_out, down_out, buf, isem, osem):
    sender = lax.axis_index("owner") * batches + lax.axis_index("batch")

    def read(i):
        g = i % owners
        at = jnp.minimum(pick_ref[g, sender], held - 1)
        src = up_ref if i < owners else down_ref
        return pltpu.make_async_copy(src.at[at], buf.at[i], isem.at[i])

    def write(i):
        dst = up_out if i < owners else down_out
        return pltpu.make_async_copy(buf.at[i], dst.at[i % owners], osem.at[i])

    for i in range(2 * owners):
        read(i).start()
    for g in range(owners):
        live = (pick_ref[g, sender] < held).astype(jnp.float32)
        live_ref[g:g + 1, :] = jnp.full((1, BLOCK), live, jnp.float32)
    for i in range(2 * owners):
        read(i).wait()
        write(i).start()
    for i in range(2 * owners):
        write(i).wait()


def fetch(owners, batches, up_rows, down_rows, pick):
    width = up_rows.shape[1]
    held = up_rows.shape[0] // BLOCK
    hbm = pl.BlockSpec(memory_space=pl.ANY)
    sent = jax.ShapeDtypeStruct((owners, BLOCK, width), up_rows.dtype)
    return pl.pallas_call(
        functools.partial(fetch_kernel, owners, batches, held),
        out_shape=(jax.ShapeDtypeStruct((owners, BLOCK), jnp.float32), sent, sent),
        in_specs=[pl.BlockSpec(memory_space=pltpu.SMEM), hbm, hbm],
        out_specs=(pl.BlockSpec(memory_space=pltpu.VMEM), hbm, hbm),
        scratch_shapes=[
            pltpu.VMEM((2 * owners, BLOCK, width), up_rows.dtype),
            pltpu.SemaphoreType.DMA((2 * owners,)),
            pltpu.SemaphoreType.DMA((2 * owners,)),
        ],
        compiler_params=pltpu.CompilerParams(vmem_limit_bytes=VMEM_BUDGET),
        name="fetch",
    )(pick, up_rows.reshape(held, BLOCK, width), down_rows.reshape(held, BLOCK, width))


def stay_body(hidden, gains, up_rows, down_rows, pick):
    owners = lax.axis_size("owner")
    batches = lax.axis_size("batch")
    live, up_send, down_send = fetch(owners, batches, up_rows, down_rows, pick)
    state = hidden
    for layer_at in range(LAYERS):
        state = run_layer(layer_at, owners, batches, state, gains, live, up_send, down_send)
    return state


def normalize(rows_in, gain_row):
    values = rows_in.astype(jnp.float32)
    row_mean = jnp.mean(values, axis=1, keepdims=True)
    centered = values - row_mean
    row_var = jnp.mean(centered * centered, axis=1, keepdims=True)
    return (centered * lax.rsqrt(row_var + 1e-05) * gain_row[None, :]).astype(jnp.bfloat16)


def body(hidden, gains, up_rows, down_rows, pick):
    owners = lax.axis_size("owner")
    batches = lax.axis_size("batch")
    group_at = lax.axis_index("owner")
    lane_at = lax.axis_index("batch")
    held_blocks = up_rows.shape[0] // BLOCK
    model_width = up_rows.shape[1]
    local_rows = hidden.shape[0]
    sender = group_at * batches + lane_at
    my_picks = lax.dynamic_slice_in_dim(pick, sender, 1, 1)[:, 0]
    chosen = jnp.minimum(my_picks, held_blocks - 1)
    up_send = up_rows.reshape(held_blocks, BLOCK, model_width)[chosen]
    down_send = down_rows.reshape(held_blocks, BLOCK, model_width)[chosen]
    group_picks = lax.dynamic_slice_in_dim(pick, group_at, 1, 0)[0]
    live_slots = (group_picks[jnp.arange(owners) * batches + lane_at] < held_blocks).astype(
        jnp.float32
    )
    up_recv, down_recv = (
        lax.all_to_all(up_send, "owner", split_axis=0, concat_axis=0, tiled=True),
        lax.all_to_all(down_send, "owner", split_axis=0, concat_axis=0, tiled=True),
    )
    per_layer = owners // LAYERS
    residual = hidden
    for layer_at in range(LAYERS):
        first_slot = layer_at * per_layer
        up_part = up_recv[first_slot : first_slot + per_layer]
        down_part = down_recv[first_slot : first_slot + per_layer]
        keep_slots = live_slots[first_slot : first_slot + per_layer]
        up_flat = up_part.reshape(per_layer * BLOCK, model_width)
        down_flat = down_part.reshape(per_layer * BLOCK, model_width)
        neuron_mask = jnp.repeat(keep_slots, BLOCK)
        normed = normalize(residual, gains[layer_at])

        def expand(
            rows_piece,
            row_start,
            up_part=up_part,
            up_flat=up_flat,
            keep_slots=keep_slots,
            neuron_mask=neuron_mask,
        ):
            pre_act = lax.dot_general(
                rows_piece, up_flat, (((1,), (1,)), ((), ())), preferred_element_type=jnp.float32
            )
            return (jnp.maximum(pre_act, 0.0) * neuron_mask[None, :]).astype(jnp.bfloat16)

        active = expand(lax.all_gather(normed, "batch", axis=0, tiled=True), jnp.int32(0))

        def contract(
            row_start,
            row_count,
            active=active,
            down_part=down_part,
            down_flat=down_flat,
            keep_slots=keep_slots,
        ):
            return jnp.dot(active, down_flat, preferred_element_type=jnp.float32)

        summed = lax.psum_scatter(
            contract(jnp.int32(0), lax.axis_size("batch") * local_rows).astype(jnp.bfloat16),
            "batch",
            scatter_dimension=0,
            tiled=True,
        ).astype(jnp.float32)
        residual = (residual.astype(jnp.float32) + summed).astype(jnp.bfloat16)
    return residual


def solution(mesh):
    in_specs = (
        P(("owner", "batch"), None),
        P(),
        P(("owner", "batch"), None),
        P(("owner", "batch"), None),
        P(),
    )
    out_specs = P(("owner", "batch"), None)
    owners, batches = mesh.shape["owner"], mesh.shape["batch"]

    def whole(hidden, gains, up_rows, down_rows, pick):
        rows = hidden.shape[0] // (owners * batches)
        plan = scratch_plan(owners, batches, rows, hidden.shape[1])
        fits = owners == 2 * LAYERS and scratch_bytes(plan) * 5 < VMEM_BUDGET * 4
        chosen = stay_body if fits else body
        return jax.shard_map(chosen, mesh=mesh, in_specs=in_specs, out_specs=out_specs, check_vma=False)(
            hidden, gains, up_rows, down_rows, pick)

    return whole
```
